32 devices in a mesh: rows: 8 (over z, core), grp: 4 (over y, x).
Axes of the slice: x: 2, y: 2, z: 4, core: 2. Of those that a mesh axis runs over, the one named last changes fastest.
Arguments:
- sorted_rows: bfloat16 [8192, 2048], P(('rows', 'grp')), may hold values from -6 to 6
- combine: bfloat16 [8192], P(('rows', 'grp')), may hold values from 0.099609375 to 1
- cotangent: bfloat16 [8192, 2048], P(('rows', 'grp')), may hold values from -6 to 6
- starts: int32 [32], P(('rows', 'grp')), may hold values from 0 to 8191, as said below
- w_gate: bfloat16 [32, 2048, 768], P(('rows', 'grp')), may hold values from -0.125 to 0.125
- w_up: bfloat16 [32, 2048, 768], P(('rows', 'grp')), may hold values from -0.125 to 0.125
- w_down: bfloat16 [32, 768, 2048], P(('rows', 'grp')), may hold values from -0.21875 to 0.21875
Outputs:
- mixed: bfloat16 [8192, 2048], P(('rows', 'grp'))
- combine_grad: bfloat16 [8192], P(('rows', 'grp'))
- input_grad: bfloat16 [8192, 2048], P(('rows', 'grp'))
- grad_gate: bfloat16 [32, 2048, 768], P(('rows', 'grp'))
- grad_up: bfloat16 [32, 2048, 768], P(('rows', 'grp'))
- grad_down: bfloat16 [32, 768, 2048], P(('rows', 'grp'))
The draws below stay inside these ranges and needn't reach their ends.
Inputs may be any that keep to these rules, and one draw needn't show every extreme that they name: starts[e] is the first sorted row of expert e; starts[0] = 0, starts[31] = 8191, and 256 * e < starts[e] < 256 * (e + 1) for e >= 1, so the rows of expert e lie in shards e and e + 1 of 256 rows, and every shard after the first begins with rows of the previous expert.
All inputs are finite; a program needn't handle non-finite values.
Results may differ from the reference program's by a relative error of at most 0.0058.
Values may be sent and summed in bfloat16 or wider, within the bound.
No kernel may reach another device: no remote copies, remote signals or barrier semaphores. Data moves between devices by JAX's collectives and lax.ppermute only.
A program may use at most 128 MiB of HBM per device.

```python
import math
import jax
import jax.numpy as jnp
from jax import lax

D = 2048
H = 768
ROW_DEV = 256
EXPERTS = 32
ROWS = 8192


def draw_starts(key, part):
    expert_pos = jnp.arange(EXPERTS, dtype=jnp.int32)
    offsets = jax.random.randint(key, (EXPERTS,), 1, ROW_DEV, dtype=jnp.int32)
    offsets = jnp.where(expert_pos == 0, jnp.zeros_like(offsets), offsets)
    offsets = jnp.where(expert_pos == EXPERTS - 1, jnp.full_like(offsets, ROW_DEV - 1), offsets)
    return (expert_pos * ROW_DEV + offsets).astype(jnp.int32)


def shard_levels(own_key, dims, shards, smallest, top_value):
    factor_of, own = 1.0, jax.random.fold_in(own_key, 6)
    for position, blocks in shards:
        heights = jnp.exp(jax.random.uniform(jax.random.fold_in(own, position), (blocks,), jnp.float32, smallest / len(shards), top_value / len(shards)))
        factor_of = factor_of * jnp.repeat(heights, dims[position] // blocks).reshape([-1 if axis == position else 1 for axis in range(len(dims))])
    return factor_of


def normal_values(key, extent, width, bound, shards=(), held_as=jnp.bfloat16):
    level = shard_levels(key, extent, shards, -0.22, 0.18) if shards else 1.0
    array = jax.random.normal(key, extent, jnp.float32) * width * level
    return jnp.minimum(jnp.maximum(array, -bound), bound).astype(held_as)


def setup_inputs(seed: int = 0) -> dict:
    key_of = jax.random.split(jax.random.key(seed), 8)
    return {
        "sorted_rows": normal_values(key_of[0], (ROWS, D), 1.0, 6.0, ((0, 32),)),
        "combine": jnp.clip(jnp.exp(math.log(1.0) - 2.306499 * jax.random.uniform(key_of[1], (ROWS,), jnp.float32) ** shard_levels(key_of[1], (ROWS,), ((0, 32),), -0.2, 0.2)), 0.099609375, 1.0).astype(jnp.bfloat16),
        "cotangent": normal_values(key_of[2], (ROWS, D), 1.0, 6.0, ((0, 32),)),
        "starts": draw_starts(jax.random.fold_in(key_of[7], 71), 0),
        "w_gate": normal_values(key_of[4], (EXPERTS, D, H), D ** -0.5, 0.125, ((0, 32),)),
        "w_up": normal_values(key_of[5], (EXPERTS, D, H), D ** -0.5, 0.125, ((0, 32),)),
        "w_down": normal_values(key_of[6], (EXPERTS, H, D), H ** -0.5, 0.21875, ((0, 32),)),
    }


def expert_forward(rows_in, combine_rows, cotan_rows, gate_w, up_w, down_w):
    gate_pre = jnp.dot(rows_in, gate_w, preferred_element_type=jnp.float32)
    up_pre = jnp.dot(rows_in, up_w, preferred_element_type=jnp.float32)
    sig_gate = jax.nn.sigmoid(gate_pre)
    silu_gate = gate_pre * sig_gate
    hidden = (silu_gate * up_pre).astype(jnp.bfloat16)
    expert_out = jnp.dot(hidden, down_w, preferred_element_type=jnp.float32)
    scale_col = combine_rows.astype(jnp.float32)[:, None]
    mixed = (scale_col * expert_out).astype(jnp.bfloat16)
    comb_grad = jnp.sum(expert_out * cotan_rows.astype(jnp.float32), axis=1).astype(jnp.bfloat16)
    out_grad = (scale_col * cotan_rows.astype(jnp.float32)).astype(jnp.bfloat16)
    return gate_pre, up_pre, sig_gate, silu_gate, hidden, mixed, comb_grad, out_grad


def expert_backward(rows_in, out_grad, gate_pre, up_pre, sig_gate, silu_gate, hidden, gate_w, up_w, down_w):
    hidden_grad = jnp.dot(out_grad, down_w.T, preferred_element_type=jnp.float32)
    gate_grad = (hidden_grad * up_pre * sig_gate * (1.0 + gate_pre * (1.0 - sig_gate))).astype(jnp.bfloat16)
    up_grad = (hidden_grad * silu_gate).astype(jnp.bfloat16)
    in_grad = (jnp.dot(gate_grad, gate_w.T, preferred_element_type=jnp.float32)
               + jnp.dot(up_grad, up_w.T, preferred_element_type=jnp.float32)).astype(jnp.bfloat16)
    gate_wgrad = jnp.dot(rows_in.T, gate_grad, preferred_element_type=jnp.float32)
    up_wgrad = jnp.dot(rows_in.T, up_grad, preferred_element_type=jnp.float32)
    down_wgrad = jnp.dot(hidden.T, out_grad, preferred_element_type=jnp.float32)
    return in_grad, gate_wgrad, up_wgrad, down_wgrad


def join_halves(first, second):
    shifted = jnp.concatenate([jnp.zeros_like(second[:1]), second[:-1]], axis=0)
    total = first + shifted
    return total.reshape((ROWS,) + total.shape[2:])


def reference(sorted_rows, combine, cotangent, starts, w_gate, w_up, w_down):
    rows_ext = jnp.concatenate([sorted_rows, jnp.zeros((ROW_DEV, D), sorted_rows.dtype)], axis=0)
    cotan_ext = jnp.concatenate([cotangent, jnp.zeros((ROW_DEV, D), cotangent.dtype)], axis=0)
    comb_ext = jnp.concatenate([combine, jnp.zeros((ROW_DEV,), combine.dtype)], axis=0)
    bounds = jnp.concatenate([starts.astype(jnp.int32), jnp.full((1,), ROWS, jnp.int32)]).astype(jnp.int32)

    def one_expert(expert):
        base = (expert * ROW_DEV).astype(jnp.int32)
        rows_in = lax.dynamic_slice_in_dim(rows_ext, base, 2 * ROW_DEV, 0)
        cotan_rows = lax.dynamic_slice_in_dim(cotan_ext, base, 2 * ROW_DEV, 0)
        comb_rows = lax.dynamic_slice_in_dim(comb_ext, base, 2 * ROW_DEV, 0)
        index_rows = base + jnp.arange(2 * ROW_DEV, dtype=jnp.int32)
        member = (index_rows >= bounds[expert]) & (index_rows < bounds[expert + 1])
        gate_w = w_gate[expert]
        up_w = w_up[expert]
        down_w = w_down[expert]
        gate_pre, up_pre, sig_gate, silu_gate, hidden, mixed, comb_grad, out_grad = expert_forward(
            rows_in, comb_rows, cotan_rows, gate_w, up_w, down_w)
        out_grad = jnp.where(member[:, None], out_grad, jnp.zeros_like(out_grad))
        in_grad, gate_wgrad, up_wgrad, down_wgrad = expert_backward(
            rows_in, out_grad, gate_pre, up_pre, sig_gate, silu_gate, hidden, gate_w, up_w, down_w)
        mixed = jnp.where(member[:, None], mixed, jnp.zeros_like(mixed))
        comb_grad = jnp.where(member, comb_grad, jnp.zeros_like(comb_grad))
        in_grad = jnp.where(member[:, None], in_grad, jnp.zeros_like(in_grad))
        return (mixed[:ROW_DEV], mixed[ROW_DEV:], comb_grad[:ROW_DEV], comb_grad[ROW_DEV:],
                in_grad[:ROW_DEV], in_grad[ROW_DEV:], gate_wgrad.astype(jnp.bfloat16),
                up_wgrad.astype(jnp.bfloat16), down_wgrad.astype(jnp.bfloat16))

    results = lax.map(one_expert, jnp.arange(EXPERTS, dtype=jnp.int32))
    mixed = join_halves(results[0], results[1])
    comb_grad = join_halves(results[2], results[3])
    in_grad = join_halves(results[4], results[5])
    return mixed, comb_grad, in_grad, results[6], results[7], results[8]
```

```python
import jax
import jax.numpy as jnp
from jax import lax
from jax.sharding import PartitionSpec as P


def from_behind(block, axis, distance):
    devices = range(lax.axis_size(axis))
    route = [(i - distance, i) for i in devices if i - distance in devices]
    return lax.ppermute(block, axis, route)


def contract_rows(left, right):
    return lax.dot_general(
        left, right, (((0,), (0,)), ((), ())), preferred_element_type=jnp.float32
    )


def contract_cols(left, right):
    return lax.dot_general(
        left, right, (((1,), (1,)), ((), ())), preferred_element_type=jnp.float32
    )


def expert_up(rows_in, gate_w, up_w):
    gate_pre = jnp.dot(rows_in, gate_w, preferred_element_type=jnp.float32)
    up_pre = jnp.dot(rows_in, up_w, preferred_element_type=jnp.float32)
    hidden = (gate_pre * jax.nn.sigmoid(gate_pre) * up_pre).astype(jnp.bfloat16)
    return lax.optimization_barrier((gate_pre, up_pre, hidden))


def expert_down(hidden, scale_col, down_w):
    expert_out = jnp.dot(hidden, down_w, preferred_element_type=jnp.float32)
    mixed = (scale_col * expert_out).astype(jnp.bfloat16)
    return lax.optimization_barrier((expert_out, mixed))


def output_grad(expert_out, scale_col, cotan_rows, keep):
    cotan_wide = cotan_rows.astype(jnp.float32)
    comb_grad = jnp.sum(expert_out * cotan_wide, axis=1).astype(jnp.bfloat16)
    out_grad = (scale_col * cotan_wide).astype(jnp.bfloat16)
    if keep is not None:
        out_grad = jnp.where(keep[:, None], out_grad, jnp.zeros_like(out_grad))
    return comb_grad, out_grad


def expert_back(out_grad, pre, gate_w, up_w, down_w):
    gate_pre, up_pre, _ = pre
    sig_gate = jax.nn.sigmoid(gate_pre)
    silu_gate = gate_pre * sig_gate
    hidden_grad = contract_cols(out_grad, down_w)
    gate_grad = (hidden_grad * up_pre * sig_gate * (1.0 + gate_pre * (1.0 - sig_gate))).astype(
        jnp.bfloat16
    )
    up_grad = (hidden_grad * silu_gate).astype(jnp.bfloat16)
    in_grad = (contract_cols(gate_grad, gate_w) + contract_cols(up_grad, up_w)).astype(jnp.bfloat16)
    return lax.optimization_barrier((gate_grad, up_grad, in_grad))


def device_step(sorted_rows, combine, cotangent, starts, w_gate, w_up, w_down):
    axes = ("rows", "grp")
    gate_w, up_w, down_w = w_gate[0], w_up[0], w_down[0]
    count_rows = sorted_rows.shape[0]
    lead_count = jnp.remainder(starts[0], count_rows)
    lead_mask = jnp.arange(count_rows, dtype=jnp.int32) < lead_count
    own_mask = jnp.logical_not(lead_mask)

    next_rows = from_behind(sorted_rows, axes, -1)
    next_comb = from_behind(jnp.where(lead_mask, combine, jnp.zeros_like(combine)), axes, -1)
    next_cotan = from_behind(cotangent, axes, -1)

    own_scale = combine.astype(jnp.float32)[:, None]
    own_pre = expert_up(sorted_rows, gate_w, up_w)
    own_out, own_mixed = expert_down(own_pre[2], own_scale, down_w)
    own_comb_grad, own_out_grad = output_grad(own_out, own_scale, cotangent, own_mask)
    own_gate_grad, own_up_grad, own_in_grad = expert_back(
        own_out_grad, own_pre, gate_w, up_w, down_w
    )

    next_scale = next_comb.astype(jnp.float32)[:, None]
    next_pre = expert_up(next_rows, gate_w, up_w)
    next_out, next_mixed = expert_down(next_pre[2], next_scale, down_w)
    back_mixed = from_behind(next_mixed, axes, 1)

    next_comb_grad, next_out_grad = output_grad(next_out, next_scale, next_cotan, None)
    next_gate_grad, next_up_grad, next_in_grad = expert_back(
        next_out_grad, next_pre, gate_w, up_w, down_w
    )
    back_comb_grad = from_behind(next_comb_grad, axes, 1)
    back_in_grad = from_behind(next_in_grad, axes, 1)

    rows_all = jnp.concatenate([sorted_rows, next_rows], axis=0)
    hidden_all = jnp.concatenate([own_pre[2], next_pre[2]], axis=0)
    out_grad_all = jnp.concatenate([own_out_grad, next_out_grad], axis=0)
    gate_grad_all = jnp.concatenate([own_gate_grad, next_gate_grad], axis=0)
    up_grad_all = jnp.concatenate([own_up_grad, next_up_grad], axis=0)
    grad_gate = contract_rows(rows_all, gate_grad_all)[None].astype(jnp.bfloat16)
    grad_up = contract_rows(rows_all, up_grad_all)[None].astype(jnp.bfloat16)
    grad_down = contract_rows(hidden_all, out_grad_all)[None].astype(jnp.bfloat16)

    mixed = jnp.where(lead_mask[:, None], back_mixed, own_mixed)
    comb_grad = jnp.where(lead_mask, back_comb_grad, own_comb_grad)
    in_grad = jnp.where(lead_mask[:, None], back_in_grad, own_in_grad)
    return (mixed, comb_grad, in_grad, grad_gate, grad_up, grad_down)


def solution(mesh):
    in_specs = (
        P(("rows", "grp"), None),
        P(("rows", "grp")),
        P(("rows", "grp"), None),
        P(("rows", "grp")),
        P(("rows", "grp"), None, None),
        P(("rows", "grp"), None, None),
        P(("rows", "grp"), None, None),
    )
    out_specs = (
        P(("rows", "grp"), None),
        P(("rows", "grp")),
        P(("rows", "grp"), None),
        P(("rows", "grp"), None, None),
        P(("rows", "grp"), None, None),
        P(("rows", "grp"), None, None),
    )
    return jax.shard_map(
        device_step, mesh=mesh, in_specs=in_specs, out_specs=out_specs, check_vma=False
    )
```

```python
import jax
import jax.numpy as jnp
from jax import lax
from jax.experimental import pallas as pl
from jax.experimental.pallas import tpu as pltpu
from jax.sharding import PartitionSpec as P


AXES = ("rows", "grp")
TAIL_SHARE = 4


def from_behind(block, distance):
    devices = range(lax.axis_size(AXES))
    route = [(i - distance, i) for i in devices if i - distance in devices]
    return lax.ppermute(block, AXES, route)


def contract_rows(left, right):
    return lax.dot_general(
        left, right, (((0,), (0,)), ((), ())), preferred_element_type=jnp.float32
    )


def contract_cols(left, right):
    return lax.dot_general(
        left, right, (((1,), (1,)), ((), ())), preferred_element_type=jnp.float32
    )


def expert_up(rows_in, gate_w, up_w):
    gate_pre = jnp.dot(rows_in, gate_w, preferred_element_type=jnp.float32)
    up_pre = jnp.dot(rows_in, up_w, preferred_element_type=jnp.float32)
    hidden = (gate_pre * jax.nn.sigmoid(gate_pre) * up_pre).astype(jnp.bfloat16)
    return lax.optimization_barrier((gate_pre, up_pre, hidden))


def expert_down(hidden, scale_col, down_w):
    expert_out = jnp.dot(hidden, down_w, preferred_element_type=jnp.float32)
    mixed = (scale_col * expert_out).astype(jnp.bfloat16)
    return lax.optimization_barrier((expert_out, mixed))


def output_grad(expert_out, scale_col, cotan_rows, keep):
    cotan_wide = cotan_rows.astype(jnp.float32)
    comb_grad = jnp.sum(expert_out * cotan_wide, axis=1).astype(jnp.bfloat16)
    out_grad = (scale_col * cotan_wide).astype(jnp.bfloat16)
    if keep is not None:
        out_grad = jnp.where(keep[:, None], out_grad, jnp.zeros_like(out_grad))
    return comb_grad, out_grad


def expert_back(out_grad, gate_pre, up_pre, gate_w, up_w, down_w):
    sig_gate = jax.nn.sigmoid(gate_pre)
    silu_gate = gate_pre * sig_gate
    hidden_grad = contract_cols(out_grad, down_w)
    gate_grad = (hidden_grad * up_pre * sig_gate * (1.0 + gate_pre * (1.0 - sig_gate))).astype(
        jnp.bfloat16
    )
    up_grad = (hidden_grad * silu_gate).astype(jnp.bfloat16)
    in_grad = (contract_cols(gate_grad, gate_w) + contract_cols(up_grad, up_w)).astype(jnp.bfloat16)
    return lax.optimization_barrier((gate_grad, up_grad, in_grad))


def join_tail(lead_count, back, own_tail, whole, start):
    rows, cols = back.shape

    def kernel(lead_ref, back_ref, own_ref, whole_ref, out_ref):
        row = start + lax.broadcasted_iota(jnp.int32, (rows, cols), 0)
        out_ref[...] = jnp.where(row < lead_ref[0], back_ref[...], own_ref[...])

    resident = pl.BlockSpec(memory_space=pltpu.VMEM)
    return pl.pallas_call(
        kernel,
        out_shape=jax.ShapeDtypeStruct(whole.shape, whole.dtype),
        grid_spec=pltpu.PrefetchScalarGridSpec(
            num_scalar_prefetch=1,
            grid=(1,),
            in_specs=[resident, resident, pl.BlockSpec(memory_space=pl.ANY)],
            out_specs=pl.BlockSpec((rows, cols), lambda i, lead: (start // rows, 0)),
        ),
        input_output_aliases={3: 0},
        name="join_tail",
    )(lead_count[None], back, own_tail, whole)


def device_step(sorted_rows, combine, cotangent, starts, w_gate, w_up, w_down):
    gate_w, up_w, down_w = w_gate[0], w_up[0], w_down[0]
    count_rows = sorted_rows.shape[0]
    cut = count_rows - count_rows // TAIL_SHARE
    pieces = [slice(0, cut), slice(cut, count_rows)]
    lead_count = jnp.remainder(starts[0], count_rows)
    lead_mask = jnp.arange(count_rows, dtype=jnp.int32) < lead_count
    own_mask = jnp.logical_not(lead_mask)

    next_rows = from_behind(sorted_rows, -1)
    next_comb = from_behind(jnp.where(lead_mask, combine, jnp.zeros_like(combine)), -1)
    next_cotan = []
    for piece in pieces:
        next_cotan.append(from_behind(cotangent[piece], -1))

    own_scale = combine.astype(jnp.float32)[:, None]
    own_gate, own_up, own_hidden = expert_up(sorted_rows, gate_w, up_w)
    own_out, own_mixed = expert_down(own_hidden, own_scale, down_w)
    own_comb_grad, own_out_grad = output_grad(own_out, own_scale, cotangent, own_mask)
    own_gate_grad, own_up_grad, own_in_grad = expert_back(
        own_out_grad, own_gate, own_up, gate_w, up_w, down_w
    )

    next_scale = next_comb.astype(jnp.float32)[:, None]
    next_gate, next_up, next_hidden = expert_up(next_rows, gate_w, up_w)
    next_out, next_mixed = expert_down(next_hidden, next_scale, down_w)
    back_mixed = from_behind(next_mixed, 1)

    next_comb_grad, next_out_grad, next_gate_grad, next_up_grad, back_in = [], [], [], [], []
    for p, piece in enumerate(pieces):
        comb_grad, out_grad = output_grad(next_out[piece], next_scale[piece], next_cotan[p], None)
        gate_grad, up_grad, in_grad = expert_back(
            out_grad, next_gate[piece], next_up[piece], gate_w, up_w, down_w
        )
        next_out, next_gate, next_up, in_grad = lax.optimization_barrier(
            (next_out, next_gate, next_up, in_grad)
        )
        next_comb_grad.append(comb_grad)
        next_out_grad.append(out_grad)
        next_gate_grad.append(gate_grad)
        next_up_grad.append(up_grad)
        back_in.append(from_behind(in_grad, 1))
    back_comb_grad = from_behind(jnp.concatenate(next_comb_grad), 1)

    rows_all = jnp.concatenate([sorted_rows, next_rows], axis=0)
    hidden_all = jnp.concatenate([own_hidden, next_hidden], axis=0)
    out_grad_all = jnp.concatenate([own_out_grad] + next_out_grad, axis=0)
    gate_grad_all = jnp.concatenate([own_gate_grad] + next_gate_grad, axis=0)
    up_grad_all = jnp.concatenate([own_up_grad] + next_up_grad, axis=0)
    grad_gate = contract_rows(rows_all, gate_grad_all)[None].astype(jnp.bfloat16)
    grad_up = contract_rows(rows_all, up_grad_all)[None].astype(jnp.bfloat16)
    grad_down = contract_rows(hidden_all, out_grad_all)[None].astype(jnp.bfloat16)

    mixed = lax.optimization_barrier(jnp.where(lead_mask[:, None], back_mixed, own_mixed))
    head, tail = pieces
    joined = jnp.where(lead_mask[head][:, None], back_in[0], own_in_grad[head])
    in_grad = lax.optimization_barrier(jnp.concatenate([joined, own_in_grad[tail]]))
    in_grad = join_tail(lead_count, back_in[1], own_in_grad[tail], in_grad, tail.start)
    comb_grad = jnp.where(lead_mask, back_comb_grad, own_comb_grad)
    return (mixed, comb_grad, in_grad, grad_gate, grad_up, grad_down)


def solution(mesh):
    rows_1d, rows_2d, rows_3d = P(AXES), P(AXES, None), P(AXES, None, None)
    return jax.shard_map(
        device_step,
        mesh=mesh,
        in_specs=(rows_2d, rows_1d, rows_2d, rows_1d, rows_3d, rows_3d, rows_3d),
        out_specs=(rows_2d, rows_1d, rows_2d, rows_3d, rows_3d, rows_3d),
        check_vma=False,
    )
```

```python
import jax
import jax.numpy as jnp
from jax import lax
from jax.sharding import PartitionSpec as P


def from_behind(block, axis, distance):
    devices = range(lax.axis_size(axis))
    route = [(i - distance, i) for i in devices if i - distance in devices]
    return lax.ppermute(block, axis, route)


def contract_rows(left, right):
    return lax.dot_general(
        left, right, (((0,), (0,)), ((), ())), preferred_element_type=jnp.float32
    )


def contract_cols(left, right):
    return lax.dot_general(
        left, right, (((1,), (1,)), ((), ())), preferred_element_type=jnp.float32
    )


def expert_up(rows_in, gate_w, up_w):
    gate_pre = jnp.dot(rows_in, gate_w, preferred_element_type=jnp.float32)
    up_pre = jnp.dot(rows_in, up_w, preferred_element_type=jnp.float32)
    hidden = (gate_pre * jax.nn.sigmoid(gate_pre) * up_pre).astype(jnp.bfloat16)
    return lax.optimization_barrier((gate_pre, up_pre, hidden))


def expert_down(hidden, scale_col, down_w):
    expert_out = jnp.dot(hidden, down_w, preferred_element_type=jnp.float32)
    mixed = (scale_col * expert_out).astype(jnp.bfloat16)
    return lax.optimization_barrier((expert_out, mixed))


def output_grad(expert_out, scale_col, cotan_rows, keep):
    cotan_wide = cotan_rows.astype(jnp.float32)
    comb_grad = jnp.sum(expert_out * cotan_wide, axis=1).astype(jnp.bfloat16)
    out_grad = (scale_col * cotan_wide).astype(jnp.bfloat16)
    if keep is not None:
        out_grad = jnp.where(keep[:, None], out_grad, jnp.zeros_like(out_grad))
    return comb_grad, out_grad


def expert_back(out_grad, pre, gate_w, up_w, down_w):
    gate_pre, up_pre, _ = pre
    sig_gate = jax.nn.sigmoid(gate_pre)
    silu_gate = gate_pre * sig_gate
    hidden_grad = contract_cols(out_grad, down_w)
    gate_grad = (hidden_grad * up_pre * sig_gate * (1.0 + gate_pre * (1.0 - sig_gate))).astype(
        jnp.bfloat16
    )
    up_grad = (hidden_grad * silu_gate).astype(jnp.bfloat16)
    in_grad = (contract_cols(gate_grad, gate_w) + contract_cols(up_grad, up_w)).astype(jnp.bfloat16)
    return lax.optimization_barrier((gate_grad, up_grad, in_grad))


def device_step(sorted_rows, combine, cotangent, starts, w_gate, w_up, w_down):
    axes = ("rows", "grp")
    gate_w, up_w, down_w = w_gate[0], w_up[0], w_down[0]
    count_rows = sorted_rows.shape[0]
    lead_count = jnp.remainder(starts[0], count_rows)
    lead_mask = jnp.arange(count_rows, dtype=jnp.int32) < lead_count
    own_mask = jnp.logical_not(lead_mask)

    next_rows = from_behind(sorted_rows, axes, -1)
    next_comb = from_behind(jnp.where(lead_mask, combine, jnp.zeros_like(combine)), axes, -1)
    next_cotan = from_behind(cotangent, axes, -1)

    own_scale = combine.astype(jnp.float32)[:, None]
    own_pre = expert_up(sorted_rows, gate_w, up_w)
    own_out, own_mixed = expert_down(own_pre[2], own_scale, down_w)
    own_comb_grad, own_out_grad = output_grad(own_out, own_scale, cotangent, own_mask)
    own_gate_grad, own_up_grad, own_in_grad = expert_back(
        own_out_grad, own_pre, gate_w, up_w, down_w
    )

    next_scale = next_comb.astype(jnp.float32)[:, None]
    next_pre = expert_up(next_rows, gate_w, up_w)
    next_out, next_mixed = expert_down(next_pre[2], next_scale, down_w)
    back_mixed = from_behind(next_mixed, axes, 1)

    next_comb_grad, next_out_grad = output_grad(next_out, next_scale, next_cotan, None)
    next_gate_grad, next_up_grad, next_in_grad = expert_back(
        next_out_grad, next_pre, gate_w, up_w, down_w
    )
    back_comb_grad = from_behind(next_comb_grad, axes, 1)
    back_in_grad = from_behind(next_in_grad, axes, 1)

    rows_all = jnp.concatenate([sorted_rows, next_rows], axis=0)
    hidden_all = jnp.concatenate([own_pre[2], next_pre[2]], axis=0)
    out_grad_all = jnp.concatenate([own_out_grad, next_out_grad], axis=0)
    gate_grad_all = jnp.concatenate([own_gate_grad, next_gate_grad], axis=0)
    up_grad_all = jnp.concatenate([own_up_grad, next_up_grad], axis=0)
    grad_gate = contract_rows(rows_all, gate_grad_all)[None].astype(jnp.bfloat16)
    grad_up = contract_rows(rows_all, up_grad_all)[None].astype(jnp.bfloat16)
    grad_down = contract_rows(hidden_all, out_grad_all)[None].astype(jnp.bfloat16)

    comb_grad = lax.optimization_barrier(jnp.where(lead_mask, back_comb_grad, own_comb_grad))
    mixed = jnp.where(lead_mask[:, None], back_mixed, own_mixed)
    mixed, own_in_grad = lax.optimization_barrier((mixed, own_in_grad))
    row = lax.broadcasted_iota(jnp.int32, own_in_grad.shape, 0)
    in_grad = jnp.where(row < lead_count, back_in_grad, own_in_grad)
    return (mixed, comb_grad, in_grad, grad_gate, grad_up, grad_down)


def solution(mesh):
    in_specs = (
        P(("rows", "grp"), None),
        P(("rows", "grp")),
        P(("rows", "grp"), None),
        P(("rows", "grp")),
        P(("rows", "grp"), None, None),
        P(("rows", "grp"), None, None),
        P(("rows", "grp"), None, None),
    )
    out_specs = (
        P(("rows", "grp"), None),
        P(("rows", "grp")),
        P(("rows", "grp"), None),
        P(("rows", "grp"), None, None),
        P(("rows", "grp"), None, None),
        P(("rows", "grp"), None, None),
    )
    return jax.shard_map(
        device_step, mesh=mesh, in_specs=in_specs, out_specs=out_specs, check_vma=False
    )
```

```python
import jax
import jax.numpy as jnp
from jax import lax
from jax.sharding import PartitionSpec as P


def from_behind(block, axis, distance):
    devices = range(lax.axis_size(axis))
    route = [(i - distance, i) for i in devices if i - distance in devices]
    return lax.ppermute(block, axis, route)


def contract_rows(left, right):
    return lax.dot_general(
        left, right, (((0,), (0,)), ((), ())), preferred_element_type=jnp.float32
    )


def contract_cols(left, right):
    return lax.dot_general(
        left, right, (((1,), (1,)), ((), ())), preferred_element_type=jnp.float32
    )


def expert_up(rows_in, gate_w, up_w):
    gate_pre = jnp.dot(rows_in, gate_w, preferred_element_type=jnp.float32)
    up_pre = jnp.dot(rows_in, up_w, preferred_element_type=jnp.float32)
    hidden = (gate_pre * jax.nn.sigmoid(gate_pre) * up_pre).astype(jnp.bfloat16)
    return lax.optimization_barrier((gate_pre, up_pre, hidden))


def expert_down(hidden, scale_col, down_w):
    expert_out = jnp.dot(hidden, down_w, preferred_element_type=jnp.float32)
    mixed = (scale_col * expert_out).astype(jnp.bfloat16)
    return lax.optimization_barrier((expert_out, mixed))


def output_grad(expert_out, scale_col, cotan_rows, keep):
    cotan_wide = cotan_rows.astype(jnp.float32)
    comb_grad = jnp.sum(expert_out * cotan_wide, axis=1).astype(jnp.bfloat16)
    out_grad = (scale_col * cotan_wide).astype(jnp.bfloat16)
    if keep is not None:
        out_grad = jnp.where(keep[:, None], out_grad, jnp.zeros_like(out_grad))
    return comb_grad, out_grad


def expert_back(out_grad, pre, gate_w, up_w, down_w):
    gate_pre, up_pre, _ = pre
    sig_gate = jax.nn.sigmoid(gate_pre)
    silu_gate = gate_pre * sig_gate
    hidden_grad = contract_cols(out_grad, down_w)
    gate_grad = (hidden_grad * up_pre * sig_gate * (1.0 + gate_pre * (1.0 - sig_gate))).astype(
        jnp.bfloat16
    )
    up_grad = (hidden_grad * silu_gate).astype(jnp.bfloat16)
    in_grad = (contract_cols(gate_grad, gate_w) + contract_cols(up_grad, up_w)).astype(jnp.bfloat16)
    return lax.optimization_barrier((gate_grad, up_grad, in_grad))


def device_step(sorted_rows, combine, cotangent, starts, w_gate, w_up, w_down):
    axes = ("rows", "grp")
    gate_w, up_w, down_w = w_gate[0], w_up[0], w_down[0]
    count_rows = sorted_rows.shape[0]
    lead_count = jnp.remainder(starts[0], count_rows)
    lead_mask = jnp.arange(count_rows, dtype=jnp.int32) < lead_count
    own_mask = jnp.logical_not(lead_mask)

    next_rows = from_behind(sorted_rows, axes, -1)
    next_comb = from_behind(jnp.where(lead_mask, combine, jnp.zeros_like(combine)), axes, -1)
    next_cotan = from_behind(cotangent, axes, -1)

    own_scale = combine.astype(jnp.float32)[:, None]
    own_pre = expert_up(sorted_rows, gate_w, up_w)
    own_out, own_mixed = expert_down(own_pre[2], own_scale, down_w)
    own_comb_grad, own_out_grad = output_grad(own_out, own_scale, cotangent, own_mask)
    own_gate_grad, own_up_grad, own_in_grad = expert_back(
        own_out_grad, own_pre, gate_w, up_w, down_w
    )

    next_scale = next_comb.astype(jnp.float32)[:, None]
    next_pre = expert_up(next_rows, gate_w, up_w)
    next_out, next_mixed = expert_down(next_pre[2], next_scale, down_w)
    back_mixed = from_behind(next_mixed, axes, 1)

    next_comb_grad, next_out_grad = output_grad(next_out, next_scale, next_cotan, None)
    next_gate_grad, next_up_grad, next_in_grad = expert_back(
        next_out_grad, next_pre, gate_w, up_w, down_w
    )
    back_comb_grad = from_behind(next_comb_grad, axes, 1)
    cut = count_rows - count_rows // TAIL_SHARE
    back_head = from_behind(next_in_grad[:cut], axes, 1)
    back_tail = from_behind(next_in_grad[cut:], axes, 1)

    rows_all = jnp.concatenate([sorted_rows, next_rows], axis=0)
    hidden_all = jnp.concatenate([own_pre[2], next_pre[2]], axis=0)
    out_grad_all = jnp.concatenate([own_out_grad, next_out_grad], axis=0)
    gate_grad_all = jnp.concatenate([own_gate_grad, next_gate_grad], axis=0)
    up_grad_all = jnp.concatenate([own_up_grad, next_up_grad], axis=0)
    grad_gate = contract_rows(rows_all, gate_grad_all)[None].astype(jnp.bfloat16)
    grad_up = contract_rows(rows_all, up_grad_all)[None].astype(jnp.bfloat16)
    grad_down = contract_rows(hidden_all, out_grad_all)[None].astype(jnp.bfloat16)

    comb_grad = lax.optimization_barrier(jnp.where(lead_mask, back_comb_grad, own_comb_grad))
    mixed = jnp.where(lead_mask[:, None], back_mixed, own_mixed)
    mixed, own_in_grad = lax.optimization_barrier((mixed, own_in_grad))
    row = lax.broadcasted_iota(jnp.int32, own_in_grad.shape, 0)
    joined = jnp.where(row[:cut] < lead_count, back_head, own_in_grad[:cut])
    in_grad = lax.optimization_barrier(lax.dynamic_update_slice(own_in_grad, joined, (0, 0)))
    joined = jnp.where(row[cut:] < lead_count, back_tail, in_grad[cut:])
    in_grad = lax.dynamic_update_slice(in_grad, joined, (cut, 0))
    return (mixed, comb_grad, in_grad, grad_gate, grad_up, grad_down)


TAIL_SHARE = 4


def solution(mesh):
    in_specs = (
        P(("rows", "grp"), None),
        P(("rows", "grp")),
        P(("rows", "grp"), None),
        P(("rows", "grp")),
        P(("rows", "grp"), None, None),
        P(("rows", "grp"), None, None),
        P(("rows", "grp"), None, None),
    )
    out_specs = (
        P(("rows", "grp"), None),
        P(("rows", "grp")),
        P(("rows", "grp"), None),
        P(("rows", "grp"), None, None),
        P(("rows", "grp"), None, None),
        P(("rows", "grp"), None, None),
    )
    return jax.shard_map(
        device_step, mesh=mesh, in_specs=in_specs, out_specs=out_specs, check_vma=False
    )
```
